256 devices in a mesh: flow: 64 (over x, y_lo, z), cross: 4 (over y_hi, core).
Axes of the slice: x: 4, y: 4 (y_hi: 2, y_lo: 2; y = y_hi * 2 + y_lo), z: 8, core: 2. Of those that a mesh axis runs over, the one named last changes fastest.
Arguments:
- particles: float32 [12288, 8, 128], P(('flow', 'cross')), may hold values from -1.5 to 48, as said below
- counts: int32 [12288], P(('flow', 'cross')), may hold values from 32 to 128, as said below
- pairs: int32 [12288, 45], P(('flow', 'cross')), may hold values from 0 to 959, as said below
Outputs:
- rates: float32 [12288, 4, 128], P(('flow', 'cross'))
The draws below stay inside these ranges and needn't reach their ends.
Inputs may be any that keep to these rules, and one draw needn't show every extreme that they name: `particles`: each block holds one cell of 1 x 2 x 2 (cells have y index in 0 to 7 and z index in 0 to 23); which cell a block holds follows one order, the same in every slab; positions lie inside their cell; density between 0.9 and 1.1, positive masses. `counts`: some block is full. `pairs`: the codes of a block name the blocks of its own cell and of its neighbour cells within one cell across (periodic) and two slabs along the flow.
All inputs are finite; a program needn't handle non-finite values.
Results may differ from the reference program's by a relative error of at most 0.0003.
Values sent between devices are 32-bit elements; how exact they have to be, the bound alone decides.
No kernel may reach another device: no remote copies, remote signals or barrier semaphores. Data moves between devices by JAX's collectives and lax.ppermute only.
A program may use at most 64 MiB of HBM per device.

```python
import math
import jax
import jax.numpy as jnp
from jax import lax

BS = 128
NB = 45
GY = 8
SLAB_BLK = 192
GZ = 24
SLABS = 64
BLOCKS_ALL = 12288


def cell_order(key):
    return jax.random.permutation(jax.random.fold_in(key, 101), SLAB_BLK).astype(jnp.int32)


def draw_pairs(key, part):
    order = cell_order(key)
    block_of_cell = jnp.argsort(order, stable=True).astype(jnp.int32)
    cell_y = order % GY
    cell_z = order // GY
    code_list = []
    for slab_rel in (-2, -1, 0, 1, 2):
        for step_y in (-1, 0, 1):
            for step_z in (-1, 0, 1):
                other_cell = jnp.mod(cell_y + step_y, GY) + GY * jnp.mod(cell_z + step_z, GZ)
                code_list.append((slab_rel + 2) * SLAB_BLK + block_of_cell[other_cell])
    codes = jnp.stack(code_list, axis=-1)
    return jnp.broadcast_to(codes[None], (SLABS, SLAB_BLK, NB)).reshape(BLOCKS_ALL, NB).astype(jnp.int32)


def draw_counts(key, part):
    values = jax.random.randint(jax.random.fold_in(key, 202), (BLOCKS_ALL,), BS // 4, BS + 1)
    chosen = jax.random.randint(jax.random.fold_in(key, 203), (), 0, BLOCKS_ALL)
    return jnp.where(jnp.arange(BLOCKS_ALL) == chosen, BS, values).astype(jnp.int32)


def draw_particles(key, part):
    order = cell_order(key)
    cells = order[jnp.arange(BLOCKS_ALL, dtype=jnp.int32) % SLAB_BLK]
    cell_y = (cells % GY).astype(jnp.float32)[:, None]
    cell_z = (cells // GY).astype(jnp.float32)[:, None]
    key_list = jax.random.split(jax.random.fold_in(key, 303), 8)
    shape = (BLOCKS_ALL, BS)
    pos_x = jax.random.uniform(key_list[0], shape, jnp.float32)
    pos_y = 2.0 * cell_y + 2.0 * jax.random.uniform(key_list[1], shape, jnp.float32)
    pos_z = 2.0 * cell_z + 2.0 * jax.random.uniform(key_list[2], shape, jnp.float32)
    vel_u = jnp.clip(0.5 * jax.random.normal(key_list[3], shape, jnp.float32), -1.5, 1.5)
    vel_v = jnp.clip(0.5 * jax.random.normal(key_list[4], shape, jnp.float32), -1.5, 1.5)
    vel_w = jnp.clip(0.5 * jax.random.normal(key_list[5], shape, jnp.float32), -1.5, 1.5)
    density = 0.9 + 0.2 * jax.random.uniform(key_list[6], shape, jnp.float32)
    mass = density * (6.4 / BS) * jnp.exp(jax.random.uniform(key_list[7], shape, jnp.float32, -0.3, 0.3))
    return jnp.stack([pos_x, pos_y, pos_z, vel_u, vel_v, vel_w, density, mass], axis=1).astype(jnp.float32)


def setup_inputs(seed: int = 0) -> dict:
    keys = jax.random.split(jax.random.key(seed), 4)
    return {
        "particles": draw_particles(jax.random.fold_in(keys[3], 71), 0),
        "counts": draw_counts(jax.random.fold_in(keys[3], 71), 0),
        "pairs": draw_pairs(jax.random.fold_in(keys[3], 71), 0),
    }


kernel_coef = 5.0 * 21.0 / (16.0 * math.pi)
eta_square = 0.01
sound_speed = 6.0
delta_coef = 0.1
visc_coef = 0.1

def wrap_gap(gap, width):
    return gap - width * jnp.floor(gap / width + 0.5)

def interact(target, target_count, sources, source_count, slab_gap, wide_y, wide_z):
    slot_ids = jnp.arange(target.shape[1], dtype=jnp.int32)
    target_live = (slot_ids < target_count).astype(jnp.float32)
    source_live = (slot_ids[None, :] < source_count[:, None]).astype(jnp.float32)

    def target_field(field):
        return target[field][None, :, None]

    def source_field(field):
        return sources[:, field][:, None, :]
    gap_x = target_field(0) - source_field(0) - slab_gap[:, None, None]
    gap_y = wrap_gap(target_field(1) - source_field(1), wide_y)
    gap_z = wrap_gap(target_field(2) - source_field(2), wide_z)
    dist_sq = gap_x * gap_x + gap_y * gap_y + gap_z * gap_z
    radius = jnp.sqrt(dist_sq + eta_square)
    kernel = kernel_coef * jnp.maximum(1.0 - 0.5 * radius, 0.0) ** 3
    volume = (sources[:, 7] / sources[:, 6] * source_live)[:, None, :]
    weight = volume * kernel
    rho_i = target_field(6)
    rho_j = source_field(6)
    closing = (target_field(3) - source_field(3)) * gap_x + (target_field(4) - source_field(4)) * gap_y + (target_field(5) - source_field(5)) * gap_z
    density_term = weight * (-rho_i * closing + 2.0 * delta_coef * sound_speed * (rho_j - rho_i) * dist_sq / (dist_sq + eta_square))
    drho = lax.optimization_barrier(jnp.sum(density_term, axis=(0, 2)))
    pressure_term = weight * (sound_speed * sound_speed * (rho_i - 1.0) + sound_speed * sound_speed * (rho_j - 1.0) - visc_coef * sound_speed * closing / (dist_sq + eta_square))
    accel_x = lax.optimization_barrier(jnp.sum(pressure_term * gap_x, axis=(0, 2))) / target[6]
    accel_y = lax.optimization_barrier(jnp.sum(pressure_term * gap_y, axis=(0, 2))) / target[6]
    accel_z = lax.optimization_barrier(jnp.sum(pressure_term * gap_z, axis=(0, 2))) / target[6]
    return jnp.stack([drho, accel_x, accel_y, accel_z]) * target_live[None, :]

def reference(particles, counts, pairs):

    def per_block(packed):
        target, target_count, pair_codes, block_id = packed
        slab_id = block_id // SLAB_BLK
        slab_rel = pair_codes // SLAB_BLK - 2
        source_ids = (jnp.mod(slab_id + slab_rel, SLABS) * SLAB_BLK + jnp.mod(pair_codes, SLAB_BLK)).astype(jnp.int32)
        sources = particles[source_ids]
        source_count = counts[source_ids]
        return interact(target, target_count, sources, source_count, slab_rel.astype(jnp.float32), 2.0 * GY, 2.0 * GZ)
    return lax.map(per_block, (particles, counts, pairs, jnp.arange(BLOCKS_ALL, dtype=jnp.int32)))
```

```python
import functools
import math

import jax
import jax.numpy as jnp
from jax import lax
from jax.experimental import pallas as pl
from jax.experimental.pallas import tpu as pltpu
from jax.sharding import PartitionSpec as P

GY = 8
OFFS = (-2, -1, 0, 1, 2)
kernel_coef = 5.0 * 21.0 / (16.0 * math.pi)
F32 = jnp.float32
BF16 = jnp.bfloat16
NT = (((1,), (1,)), ((), ()))
GROUP = 4
PIECE = 32
ROWS = 128


def passed_along(value, axis, steps):
    count = lax.axis_size(axis)
    pairs = [(source, (source + steps) % count) for source in range(count)]
    return lax.ppermute(value, axis, pairs)


def split2(value):
    high = value.astype(BF16).astype(F32)
    return high, value - high


def split3(value):
    high, rest = split2(value)
    mid, low = split2(rest)
    return high, mid, low


def three_sum(value):
    return value[0:1] + value[1:2] + value[2:3]


def rows8():
    return lax.broadcasted_iota(jnp.int32, (8, ROWS), 0)


def lane_features(field):
    row = rows8()
    high, mid = split2(field)
    velocity = pltpu.roll(field, 5, 0)
    norm = jnp.broadcast_to(three_sum(field * field), (8, ROWS))
    cross = jnp.broadcast_to(three_sum(field * velocity), (8, ROWS))
    nh, nm, nl = split3(norm)
    bh, bm, bl = split3(cross)
    xh = jnp.where(row < 3, high, pltpu.roll(high, 3, 0))
    xm = jnp.where(row < 3, mid, pltpu.roll(mid, 3, 0))
    uh = jnp.where(row < 3, pltpu.roll(high, 5, 0), 0.0)
    um = jnp.where(row < 3, pltpu.roll(mid, 5, 0), 0.0)

    def with_tail(body, six, seven):
        return jnp.where(row == 6, six, jnp.where(row == 7, seven, body))

    features = jnp.concatenate(
        [
            with_tail(xh, 1.0, 1.0),
            with_tail(xm, 1.0, nh),
            with_tail(xh, nm, nl),
            with_tail(xm, bh, bm),
            with_tail(uh, bl, 0.0),
            um,
            uh,
            jnp.zeros((8, ROWS), F32),
        ],
        axis=0,
    )
    volume = jnp.broadcast_to(field[7:8], (8, ROWS))
    density = jnp.broadcast_to(field[6:7], (8, ROWS))
    plain = jnp.where(row == 7, volume, field * volume)
    second_set = jnp.where(row < 3, plain * density, cross * volume)
    ph, pm = split2(plain)
    sh, sm = split2(second_set)
    weights = jnp.concatenate([ph, pm, sh, sm], axis=0)
    return features.T.astype(BF16), weights.astype(BF16)


def row_features(field, frame):
    row = rows8()
    step_y, step_z = 2.0 * (frame // 3 - 1), 2.0 * (frame % 3 - 1)
    field = field - jnp.where(row == 1, step_y, jnp.where(row == 2, step_z, 0.0))
    high, mid = split2(field)
    velocity = pltpu.roll(field, 5, 0)
    norm = jnp.broadcast_to((three_sum(field * field) + 0.01) * 0.25, (8, ROWS))
    cross = jnp.broadcast_to(three_sum(field * velocity), (8, ROWS))
    nh, nm, nl = split3(norm)
    ah, am, al = split3(cross)
    first = jnp.where(row < 3, -0.5, 0.0)
    second = jnp.where((row >= 3) & (row < 6), -1.0, 0.0)
    third = jnp.where(row < 3, -1.0, 0.0)
    hf, mf = high * first, mid * first
    hs, ms = high * second, mid * second
    ht, mt = high * third, mid * third
    near = jnp.concatenate(
        [
            jnp.where(row == 6, nh, jnp.where(row == 7, nm, hf)),
            jnp.where(row == 6, nl, jnp.where(row == 7, 0.25, hf)),
            jnp.where(row >= 6, 0.25, mf),
            mf,
        ],
        axis=0,
    )
    closing = jnp.concatenate(
        [
            jnp.where(row == 6, ah, jnp.where(row == 7, am, hs)),
            jnp.where(row == 6, al, hs),
            ms,
            jnp.where(row >= 6, 1.0, ms),
            jnp.where(row == 6, 1.0, ht),
            ht,
            mt,
            jnp.zeros((8, ROWS), F32),
        ],
        axis=0,
    )
    return near.astype(BF16), closing.astype(BF16)


def kernel(blocks, slab_blk, own_count, offset, chunk_count, column,
           own_ref, raw_ref, out_ref, source, weight, near, closing, packed, pre, pairk, paird, acc_k, acc_e, acc_d):
    lane8 = lax.broadcasted_iota(jnp.int32, (8, ROWS), 1)
    row = rows8()

    def make_targets(t, carry):
        field = own_ref[t]
        for frame in range(9):
            near[t * 9 + frame], closing[t * 9 + frame] = row_features(field, frame)
        return carry

    lax.fori_loop(0, blocks, make_targets, 0)

    def make_sources(c, carry):
        base = (c // blocks) * (5 * (blocks + 1)) + c % blocks
        for order, slab in enumerate(OFFS):
            field = raw_ref[base + order * (blocks + 1)]
            field = field + jnp.where(row == 0, float(slab), 0.0)
            start = offset[order * slab_blk + c]
            inside = lax.rem(start, ROWS)
            slot = lax.div(start, ROWS)
            turned = pltpu.roll(field, inside, 1)
            here = lane8 >= inside
            packed[slot] = jnp.where(here, turned, packed[slot])
            packed[slot + 1] = jnp.where(here, 0.0, turned)

        def build(k):
            source[c * 5 + k], weight[c * 5 + k] = lane_features(packed[k])

        for k in range(3):
            build(k)

        @pl.when(chunk_count[c] > 3)
        def _():
            build(3)
            build(4)

        return carry

    packed[...] = jnp.zeros_like(packed)
    lax.fori_loop(0, slab_blk, make_sources, 0)

    acc_k[...] = jnp.zeros_like(acc_k)
    acc_e[...] = jnp.zeros_like(acc_e)
    acc_d[...] = jnp.zeros_like(acc_d)

    frame9 = lax.broadcasted_iota(jnp.int32, (9, ROWS), 0)
    shift_y = (2 * (frame9 // 3 - 1)).astype(F32)
    shift_z = (2 * (frame9 % 3 - 1)).astype(F32)
    zero_near = jnp.zeros((32, ROWS), BF16)
    zero_weight = jnp.zeros((16, ROWS), BF16)

    def finish(t):
        half = lax.rem(t, 2)
        field = own_ref[t]

        def from_k(m):
            at = half * 288 + m
            return acc_k[pl.ds(at, 9, stride=32), :] + acc_k[pl.ds(at + 8, 9, stride=32), :]

        def from_e(m):
            at = half * 288 + m
            return acc_e[pl.ds(at, 9, stride=32), :] + acc_e[pl.ds(at + 8, 9, stride=32), :]

        def from_d(m):
            at = half * 144 + m
            return acc_d[pl.ds(at, 9, stride=16), :] + acc_d[pl.ds(at + 8, 9, stride=16), :]

        def wide(m):
            return jnp.broadcast_to(field[m:m + 1], (9, ROWS))

        place = [wide(0), wide(1) - shift_y, wide(2) - shift_z]
        speed = [wide(3), wide(4), wide(5)]
        excess = wide(6)
        s_0, s_rho, s_cross = from_k(7), from_k(6), from_k(19)
        s_x = [from_k(a) for a in range(3)]
        s_u = [from_k(3 + a) for a in range(3)]
        s_rx = [from_k(16 + a) for a in range(3)]
        e_0 = from_e(7)
        e_x = [from_e(a) for a in range(3)]
        d_0, d_rho = from_d(7), from_d(6)
        own_cross = place[0] * speed[0] + place[1] * speed[1] + place[2] * speed[2]
        close = own_cross * s_0 + s_cross
        for a in range(3):
            close = close - speed[a] * s_x[a] - place[a] * s_u[a]
        spread = (s_rho - excess * s_0) - 0.0025 * (d_rho - excess * d_0)
        results = [-(1.0 + excess) * close + 1.2 * spread]
        for a in range(3):
            pressure = excess * (place[a] * s_0 - s_x[a]) + place[a] * s_rho - s_rx[a]
            viscous = place[a] * e_0 - e_x[a]
            results.append(36.0 * pressure - 0.15 * viscous)
        live = lax.broadcasted_iota(jnp.int32, (1, ROWS), 1) < own_count[t]
        rho = 1.0 + field[6:7]
        for a in range(4):
            value = kernel_coef * jnp.sum(results[a], axis=0, keepdims=True)
            value = value if a == 0 else value / rho
            out_ref[t, a:a + 1, :] = jnp.where(live, value, 0.0)
        at = pl.multiple_of(half * 288, 32)
        acc_k[pl.ds(at, 288), :] = jnp.zeros((288, ROWS), F32)
        acc_e[pl.ds(at, 288), :] = jnp.zeros((288, ROWS), F32)
        at = pl.multiple_of(half * 144, 16)
        acc_d[pl.ds(at, 144), :] = jnp.zeros((144, ROWS), F32)

    def phase(state, side):
        t, f, k, mids, olds = state
        news = []
        for u in range(GROUP):
            slot, where, _ = olds[u]
            w = weight[where]
            total = jnp.dot(jnp.concatenate([w, w], axis=1), pairk[1 - side, u], preferred_element_type=F32)
            at = pl.multiple_of(slot * 32, 32)
            acc_k[pl.ds(at, 32), :] += total[:, 0:ROWS]
            acc_e[pl.ds(at, 32), :] += total[:, ROWS:2 * ROWS]
            if u % 2:
                before = weight[olds[u - 1][1]]
                both = jnp.concatenate(
                    [
                        jnp.concatenate([before[0:16], zero_weight], axis=1),
                        jnp.concatenate([zero_weight, w[0:16]], axis=1),
                    ],
                    axis=0,
                )
                total = jnp.dot(both, paird[1 - side, u // 2], preferred_element_type=F32)
                at = pl.multiple_of(olds[u - 1][0] * 16, 16)
                acc_d[pl.ds(at, 16), :] += total[0:16]
                at = pl.multiple_of(slot * 16, 16)
                acc_d[pl.ds(at, 16), :] += total[16:32]
            inside = jnp.minimum(t, blocks - 1)
            c = column[inside * 9 + f]
            where = c * 5 + k
            frame = inside * 9 + f
            right = jnp.concatenate(
                [jnp.concatenate([near[frame], zero_near], axis=0), closing[frame]], axis=1
            )
            pre[1 - side, u] = jnp.dot(source[where], right, preferred_element_type=F32)
            news.append((jnp.where(t < blocks, lax.rem(t, 2) * 9 + f, 18), where, t))
            done = k + 1 >= chunk_count[c]
            k = jnp.where(done, 0, k + 1)
            f = jnp.where(done, f + 1, f)
            over = f > 8
            t = jnp.where(over, jnp.minimum(t + 1, blocks), t)
            f = jnp.where(over, 0, f)
            for low in range(0, ROWS, PIECE):
                part = slice(low, low + PIECE)
                rest = slice(ROWS + low, ROWS + low + PIECE)
                s = pre[side, u, part, 0:ROWS]
                e = pre[side, u, part, ROWS:2 * ROWS]
                inv = lax.rsqrt(s)
                w = jnp.maximum(1.0 - s * inv, 0.0)
                cube = w * w * w
                near_k = cube * (inv * inv)
                damp = near_k * e
                kh = cube.astype(BF16)
                dh = damp.astype(BF16)
                pairk[side, u, part, 0:ROWS] = kh
                pairk[side, u, rest, 0:ROWS] = (cube - kh.astype(F32)).astype(BF16)
                pairk[side, u, part, ROWS:2 * ROWS] = dh
                pairk[side, u, rest, ROWS:2 * ROWS] = (damp - dh.astype(F32)).astype(BF16)
                half = (u % 2) * ROWS + low
                paird[side, u // 2, half:half + PIECE] = near_k.astype(BF16)
        return t, f, k, tuple(news), mids

    def step(state):
        for side in range(2):
            mids, olds = state[3], state[4]
            state = phase(state, side)

            @pl.when(mids[0][2] > olds[0][2])
            def _():
                finish(olds[0][2])

        return state

    zero = jnp.int32(0)
    idle = tuple((jnp.int32(18), zero, zero) for _ in range(GROUP))
    lax.while_loop(lambda state: state[4][0][2] < blocks, step, (zero, zero, zero, idle, idle))


def pair_sums(own, raw, own_count, offset, chunk_count, column):
    blocks = own.shape[0]
    slab_blk = chunk_count.shape[0]
    chunks = slab_blk * 5
    smem = pl.BlockSpec(memory_space=pltpu.SMEM)
    vmem = pl.BlockSpec(memory_space=pltpu.VMEM)
    return pl.pallas_call(
        functools.partial(kernel, blocks, slab_blk),
        out_shape=jax.ShapeDtypeStruct((blocks, 4, ROWS), F32),
        in_specs=[smem] * 4 + [vmem] * 2,
        out_specs=vmem,
        scratch_shapes=[
            pltpu.VMEM((chunks, ROWS, 64), BF16),
            pltpu.VMEM((chunks, 32, ROWS), BF16),
            pltpu.VMEM((blocks * 9, 32, ROWS), BF16),
            pltpu.VMEM((blocks * 9, 64, ROWS), BF16),
            pltpu.VMEM((7, 8, ROWS), F32),
            pltpu.VMEM((2, GROUP, ROWS, 2 * ROWS), F32),
            pltpu.VMEM((2, GROUP, 2 * ROWS, 2 * ROWS), BF16),
            pltpu.VMEM((2, GROUP // 2, 2 * ROWS, ROWS), BF16),
            pltpu.VMEM((19 * 32, ROWS), F32),
            pltpu.VMEM((19 * 32, ROWS), F32),
            pltpu.VMEM((19 * 16, ROWS), F32),
        ],
        name="pair_sums",
    )(own_count, offset, chunk_count, column, own, raw)


def localize(particles, counts):
    slots = particles.shape[2]
    live = lax.broadcasted_iota(jnp.int32, (1, slots), 1) < counts[:, None]
    lowest = jnp.min(jnp.where(live[:, None], particles[:, 1:3], 1e9), axis=2)
    cell = jnp.floor(lowest * 0.5)
    centre = 2.0 * cell + 1.0
    fields = jnp.stack(
        [
            particles[:, 0] - 0.5,
            particles[:, 1] - centre[:, 0:1],
            particles[:, 2] - centre[:, 1:2],
            particles[:, 3],
            particles[:, 4],
            particles[:, 5],
            particles[:, 6] - 1.0,
            particles[:, 7] / particles[:, 6],
        ],
        axis=1,
    )
    return jnp.where(live[:, None], fields, 0.0), cell


def tables(cell, counts, cells_y, cells_z, listed, own_cell):
    starts = [jnp.zeros_like(counts[0])]
    for order in range(5):
        starts.append(starts[-1] + counts[order])
    offset = jnp.concatenate(starts[:5])
    chunk_count = (starts[5] + (ROWS - 1)) // ROWS
    frame = jnp.arange(9, dtype=jnp.int32)
    want_y = (own_cell[:, 0:1] + (frame // 3 - 1)[None] + cells_y) % cells_y
    want_z = (own_cell[:, 1:2] + (frame % 3 - 1)[None] + cells_z) % cells_z
    want = want_y + cells_y * want_z
    have = cell[0] + cells_y * cell[1]
    hit = (want[:, :, None] == have[None, None, :]) & listed[:, None, :]
    ids = jnp.arange(have.shape[0], dtype=jnp.int32)
    column = jnp.sum(jnp.where(hit, ids[None, None], 0), axis=2).astype(jnp.int32)
    return offset, chunk_count, column.reshape(-1)


def per_device(particles, counts, pairs):
    blocks = particles.shape[0]
    cross = lax.axis_size("cross")
    slab_blk = blocks * cross
    cells_z = slab_blk // GY
    local, own_cell = localize(particles, counts)
    listed = jnp.any(pairs[:, :, None] - 2 * slab_blk == jnp.arange(slab_blk, dtype=jnp.int32), axis=1)
    notes = jnp.concatenate([own_cell.T, counts[None].astype(F32), jnp.zeros((5, blocks), F32)], axis=0)
    notes = jnp.pad(notes, ((0, 0), (0, ROWS - blocks)))
    shipped = jnp.concatenate([local, notes[None]], axis=0)
    nearby = [shipped if slab == 0 else passed_along(shipped, "flow", -slab) for slab in OFFS]
    gathered = lax.all_gather(jnp.stack(nearby), "cross", axis=0)
    meta = gathered[:, :, blocks, 0:3, :blocks].astype(jnp.int32)
    meta = jnp.transpose(meta, (1, 2, 0, 3)).reshape(5, 3, slab_blk)
    offset, chunk_count, column = tables(
        (meta[2, 0], meta[2, 1]), meta[:, 2], GY, cells_z, listed, own_cell.astype(jnp.int32)
    )
    raw = gathered.reshape((cross * 5 * (blocks + 1),) + local.shape[1:])
    return pair_sums(local, raw, counts, offset, chunk_count, column)


def solution(mesh):
    placed = (P(("flow", "cross"), None, None), P(("flow", "cross")), P(("flow", "cross"), None))
    return jax.shard_map(
        per_device,
        mesh=mesh,
        in_specs=placed,
        out_specs=P(("flow", "cross"), None, None),
        check_vma=False,
    )
```

```python
import functools
import math

import jax
import jax.numpy as jnp
from jax import lax
from jax.experimental import pallas as pl
from jax.experimental.pallas import tpu as pltpu
from jax.sharding import PartitionSpec as P

GY = 8
OFFS = (-2, -1, 0, 1, 2)
kernel_coef = 5.0 * 21.0 / (16.0 * math.pi)
F32 = jnp.float32
BF16 = jnp.bfloat16
NT = (((1,), (1,)), ((), ()))
GROUP = 8
HEAD = 2
TOGETHER = 4
PIECE = 32
ROWS = 128


def passed_along(value, axis, steps):
    count = lax.axis_size(axis)
    pairs = [(source, (source + steps) % count) for source in range(count)]
    return lax.ppermute(value, axis, pairs)


def split2(value):
    high = value.astype(BF16).astype(F32)
    return high, value - high


def split3(value):
    high, rest = split2(value)
    mid, low = split2(rest)
    return high, mid, low


def three_sum(value):
    return value[0:1] + value[1:2] + value[2:3]


def rows8():
    return lax.broadcasted_iota(jnp.int32, (8, ROWS), 0)


def lane_features(field):
    row = rows8()
    high, mid = split2(field)
    velocity = pltpu.roll(field, 5, 0)
    norm = jnp.broadcast_to(three_sum(field * field), (8, ROWS))
    cross = jnp.broadcast_to(three_sum(field * velocity), (8, ROWS))
    nh, nm, nl = split3(norm)
    bh, bm, bl = split3(cross)
    xh = jnp.where(row < 3, high, pltpu.roll(high, 3, 0))
    xm = jnp.where(row < 3, mid, pltpu.roll(mid, 3, 0))
    uh = jnp.where(row < 3, pltpu.roll(high, 5, 0), 0.0)
    um = jnp.where(row < 3, pltpu.roll(mid, 5, 0), 0.0)

    def with_tail(body, six, seven):
        return jnp.where(row == 6, six, jnp.where(row == 7, seven, body))

    features = jnp.concatenate(
        [
            with_tail(xh, 1.0, 1.0),
            with_tail(xm, 1.0, nh),
            with_tail(xh, nm, nl),
            with_tail(xm, bh, bm),
            with_tail(uh, bl, 0.0),
            um,
            uh,
            jnp.zeros((8, ROWS), F32),
        ],
        axis=0,
    )
    volume = jnp.broadcast_to(field[7:8], (8, ROWS))
    density = jnp.broadcast_to(field[6:7], (8, ROWS))
    plain = jnp.where(row == 7, volume, field * volume)
    second_set = jnp.where(row < 3, plain * density, cross * volume)
    ph, pm = split2(plain)
    sh, sm = split2(second_set)
    weights = jnp.concatenate([ph, pm, sh, sm], axis=0)
    return features.T.astype(BF16), weights.astype(BF16)


def row_features(field, frame):
    row = rows8()
    step_y, step_z = 2.0 * (frame // 3 - 1), 2.0 * (frame % 3 - 1)
    field = field - jnp.where(row == 1, step_y, jnp.where(row == 2, step_z, 0.0))
    high, mid = split2(field)
    velocity = pltpu.roll(field, 5, 0)
    norm = jnp.broadcast_to((three_sum(field * field) + 0.01) * 0.25, (8, ROWS))
    cross = jnp.broadcast_to(three_sum(field * velocity), (8, ROWS))
    nh, nm, nl = split3(norm)
    ah, am, al = split3(cross)
    first = jnp.where(row < 3, -0.5, 0.0)
    second = jnp.where((row >= 3) & (row < 6), -1.0, 0.0)
    third = jnp.where(row < 3, -1.0, 0.0)
    hf, mf = high * first, mid * first
    hs, ms = high * second, mid * second
    ht, mt = high * third, mid * third
    near = jnp.concatenate(
        [
            jnp.where(row == 6, nh, jnp.where(row == 7, nm, hf)),
            jnp.where(row == 6, nl, jnp.where(row == 7, 0.25, hf)),
            jnp.where(row >= 6, 0.25, mf),
            mf,
        ],
        axis=0,
    )
    closing = jnp.concatenate(
        [
            jnp.where(row == 6, ah, jnp.where(row == 7, am, hs)),
            jnp.where(row == 6, al, hs),
            ms,
            jnp.where(row >= 6, 1.0, ms),
            jnp.where(row == 6, 1.0, ht),
            ht,
            mt,
            jnp.zeros((8, ROWS), F32),
        ],
        axis=0,
    )
    return near.astype(BF16), closing.astype(BF16)


def kernel(blocks, slab_blk, own_count, offset, chunk_count, column,
           own_ref, far_ref, back_ref, here_ref, ahead_ref, out_ref, source, weight, near, closing, *scratch):
    packs, (pre, pair_k, pair_e, pair_d, acc_k, acc_e, acc_d) = scratch[:TOGETHER], scratch[TOGETHER:]
    lane8 = lax.broadcasted_iota(jnp.int32, (8, ROWS), 1)
    row = rows8()

    def make_targets(t, carry):
        field = own_ref[t]
        for frame in range(9):
            near[t * 9 + frame], closing[t * 9 + frame] = row_features(field, frame)
        return carry

    lax.fori_loop(0, blocks, make_targets, 0)

    def make_sources(n, carry):
        firsts = [n * TOGETHER + m for m in range(TOGETHER)]
        for order, slab in enumerate(OFFS):
            for c, packed in zip(firsts, packs):
                part, place = lax.div(c, blocks), lax.rem(c, blocks)
                if slab in (-2, 2):
                    field = far_ref[(2 * part + (slab > 0)) * (blocks + 1) + place]
                else:
                    raw_ref = (back_ref, here_ref, ahead_ref)[slab + 1]
                    field = raw_ref[part * (blocks + 1) + place]
                field = field + jnp.where(row == 0, float(slab), 0.0)
                start = offset[order * slab_blk + c]
                inside = lax.rem(start, ROWS)
                slot = lax.div(start, ROWS)
                turned = pltpu.roll(field, inside, 1)
                here = lane8 >= inside
                packed[slot] = jnp.where(here, turned, packed[slot])
                packed[slot + 1] = jnp.where(here, 0.0, turned)

        def build(c, packed, k):
            source[c * 5 + k], weight[c * 5 + k] = lane_features(packed[k])

        for k in range(3):
            for c, packed in zip(firsts, packs):
                build(c, packed, k)

        for c, packed in zip(firsts, packs):
            @pl.when(chunk_count[c] > 3)
            def _():
                build(c, packed, 3)
                build(c, packed, 4)

        return carry

    for packed in packs:
        packed[...] = jnp.zeros_like(packed)
    lax.fori_loop(0, slab_blk // TOGETHER, make_sources, 0)

    pre[...] = jnp.ones_like(pre)
    pair_k[...] = jnp.zeros_like(pair_k)
    pair_e[...] = jnp.zeros_like(pair_e)
    pair_d[...] = jnp.zeros_like(pair_d)
    acc_k[...] = jnp.zeros_like(acc_k)
    acc_e[...] = jnp.zeros_like(acc_e)
    acc_d[...] = jnp.zeros_like(acc_d)

    frame9 = lax.broadcasted_iota(jnp.int32, (9, ROWS), 0)
    shift_y = (2 * (frame9 // 3 - 1)).astype(F32)
    shift_z = (2 * (frame9 % 3 - 1)).astype(F32)
    zero_near = jnp.zeros((32, ROWS), BF16)
    zero_weight = jnp.zeros((16, ROWS), BF16)

    def finish(t):
        half = lax.rem(t, 2)
        field = own_ref[t]

        def from_k(m):
            at = half * 288 + m
            return acc_k[pl.ds(at, 9, stride=32), :] + acc_k[pl.ds(at + 8, 9, stride=32), :]

        def from_e(m):
            at = half * 288 + m
            return acc_e[pl.ds(at, 9, stride=32), :] + acc_e[pl.ds(at + 8, 9, stride=32), :]

        def from_d(m):
            at = half * 144 + m
            return acc_d[pl.ds(at, 9, stride=16), :] + acc_d[pl.ds(at + 8, 9, stride=16), :]

        def wide(m):
            return jnp.broadcast_to(field[m:m + 1], (9, ROWS))

        place = [wide(0), wide(1) - shift_y, wide(2) - shift_z]
        speed = [wide(3), wide(4), wide(5)]
        excess = wide(6)
        s_0, s_rho, s_cross = from_k(7), from_k(6), from_k(19)
        s_x = [from_k(a) for a in range(3)]
        s_u = [from_k(3 + a) for a in range(3)]
        s_rx = [from_k(16 + a) for a in range(3)]
        e_0 = from_e(7)
        e_x = [from_e(a) for a in range(3)]
        d_0, d_rho = from_d(7), from_d(6)
        own_cross = place[0] * speed[0] + place[1] * speed[1] + place[2] * speed[2]
        close = own_cross * s_0 + s_cross
        for a in range(3):
            close = close - speed[a] * s_x[a] - place[a] * s_u[a]
        spread = (s_rho - excess * s_0) - 0.0025 * (d_rho - excess * d_0)
        results = [-(1.0 + excess) * close + 1.2 * spread]
        for a in range(3):
            pressure = excess * (place[a] * s_0 - s_x[a]) + place[a] * s_rho - s_rx[a]
            viscous = place[a] * e_0 - e_x[a]
            results.append(36.0 * pressure - 0.15 * viscous)
        live = lax.broadcasted_iota(jnp.int32, (1, ROWS), 1) < own_count[t]
        rho = 1.0 + field[6:7]
        for a in range(4):
            value = kernel_coef * jnp.sum(results[a], axis=0, keepdims=True)
            value = value if a == 0 else value / rho
            out_ref[t, a:a + 1, :] = jnp.where(live, value, 0.0)
        at = pl.multiple_of(half * 288, 32)
        acc_k[pl.ds(at, 288), :] = jnp.zeros((288, ROWS), F32)
        acc_e[pl.ds(at, 288), :] = jnp.zeros((288, ROWS), F32)
        at = pl.multiple_of(half * 144, 16)
        acc_d[pl.ds(at, 144), :] = jnp.zeros((144, ROWS), F32)

    def phase(state, side):
        t, f, k, heads, olds = state

        def advance():
            nonlocal t, f, k
            inside = jnp.minimum(t, blocks - 1)
            c = column[inside * 9 + f]
            where = c * 5 + k
            frame = inside * 9 + f
            right = jnp.concatenate(
                [jnp.concatenate([near[frame], zero_near], axis=0), closing[frame]], axis=1
            )
            both_ends = jnp.dot(source[where], right, preferred_element_type=F32)
            item = (jnp.where(t < blocks, lax.rem(t, 2) * 9 + f, 18), where, t)
            done = k + 1 >= chunk_count[c]
            k = jnp.where(done, 0, k + 1)
            f = jnp.where(done, f + 1, f)
            over = f > 8
            t = jnp.where(over, jnp.minimum(t + 1, blocks), t)
            f = jnp.where(over, 0, f)
            return both_ends, item

        news = list(heads)
        for u in range(GROUP):
            if u < HEAD:
                both_ends = pre[side, u]
            else:
                both_ends, item = advance()
                news.append(item)
            for low in range(0, ROWS, PIECE):
                part = slice(low, low + PIECE)
                rest = slice(ROWS + low, ROWS + low + PIECE)
                s = both_ends[part, 0:ROWS]
                e = both_ends[part, ROWS:2 * ROWS]
                inv = lax.rsqrt(s)
                w = jnp.maximum(1.0 - s * inv, 0.0)
                cube = w * w * w
                near_k = cube * (inv * inv)
                damp = near_k * e
                kh = cube.astype(BF16)
                dh = damp.astype(BF16)
                pair_k[side, u, part] = kh
                pair_k[side, u, rest] = (cube - kh.astype(F32)).astype(BF16)
                pair_e[side, u, part] = dh
                pair_e[side, u, rest] = (damp - dh.astype(F32)).astype(BF16)
                half = (u % 2) * ROWS + low
                pair_d[side, u // 2, half:half + PIECE] = near_k.astype(BF16)
            slot, where, _ = olds[u]
            w = weight[where]
            right = jnp.concatenate([pair_k[1 - side, u], pair_e[1 - side, u]], axis=1)
            total = jnp.dot(jnp.concatenate([w, w], axis=1), right, preferred_element_type=F32)
            at = pl.multiple_of(slot * 32, 32)
            acc_k[pl.ds(at, 32), :] += total[:, 0:ROWS]
            acc_e[pl.ds(at, 32), :] += total[:, ROWS:2 * ROWS]
            if u % 2:
                before = weight[olds[u - 1][1]]
                both = jnp.concatenate(
                    [
                        jnp.concatenate([before[0:16], zero_weight], axis=1),
                        jnp.concatenate([zero_weight, w[0:16]], axis=1),
                    ],
                    axis=0,
                )
                total = jnp.dot(both, pair_d[1 - side, u // 2], preferred_element_type=F32)
                at = pl.multiple_of(olds[u - 1][0] * 16, 16)
                acc_d[pl.ds(at, 16), :] += total[0:16]
                at = pl.multiple_of(slot * 16, 16)
                acc_d[pl.ds(at, 16), :] += total[16:32]
        heads = []
        for u in range(HEAD):
            both_ends, item = advance()
            pre[1 - side, u] = both_ends
            heads.append(item)
        return t, f, k, tuple(heads), tuple(news)

    def step(state):
        for side in range(2):
            olds = state[4]
            state = phase(state, side)

            @pl.when(state[4][0][2] > olds[0][2])
            def _():
                finish(olds[0][2])

        return state

    zero = jnp.int32(0)
    idle = tuple((jnp.int32(18), zero, zero) for _ in range(GROUP))
    lax.while_loop(lambda state: state[4][0][2] < blocks, step, (zero, zero, zero, idle[:HEAD], idle))


def pair_sums(own, raws, own_count, offset, chunk_count, column):
    blocks = own.shape[0]
    slab_blk = chunk_count.shape[0]
    chunks = slab_blk * 5
    smem = pl.BlockSpec(memory_space=pltpu.SMEM)
    vmem = pl.BlockSpec(memory_space=pltpu.VMEM)
    return pl.pallas_call(
        functools.partial(kernel, blocks, slab_blk),
        out_shape=jax.ShapeDtypeStruct((blocks, 4, ROWS), F32),
        in_specs=[smem] * 4 + [vmem] * 5,
        out_specs=vmem,
        scratch_shapes=[
            pltpu.VMEM((chunks, ROWS, 64), BF16),
            pltpu.VMEM((chunks, 32, ROWS), BF16),
            pltpu.VMEM((blocks * 9, 32, ROWS), BF16),
            pltpu.VMEM((blocks * 9, 64, ROWS), BF16),
            *[pltpu.VMEM((7, 8, ROWS), F32) for _ in range(TOGETHER)],
            pltpu.VMEM((2, HEAD, ROWS, 2 * ROWS), F32),
            pltpu.VMEM((2, GROUP, 2 * ROWS, ROWS), BF16),
            pltpu.VMEM((2, GROUP, 2 * ROWS, ROWS), BF16),
            pltpu.VMEM((2, GROUP // 2, 2 * ROWS, ROWS), BF16),
            pltpu.VMEM((19 * 32, ROWS), F32),
            pltpu.VMEM((19 * 32, ROWS), F32),
            pltpu.VMEM((19 * 16, ROWS), F32),
        ],
        name="pair_sums",
    )(own_count, offset, chunk_count, column, own, *raws)


def localize(particles, counts):
    slots = particles.shape[2]
    live = lax.broadcasted_iota(jnp.int32, (1, slots), 1) < counts[:, None]
    lowest = jnp.min(jnp.where(live[:, None], particles[:, 1:3], 1e9), axis=2)
    cell = jnp.floor(lowest * 0.5)
    centre = 2.0 * cell + 1.0
    fields = jnp.stack(
        [
            particles[:, 0] - 0.5,
            particles[:, 1] - centre[:, 0:1],
            particles[:, 2] - centre[:, 1:2],
            particles[:, 3],
            particles[:, 4],
            particles[:, 5],
            particles[:, 6] - 1.0,
            particles[:, 7] / particles[:, 6],
        ],
        axis=1,
    )
    return jnp.where(live[:, None], fields, 0.0), cell


def tables(cell, counts, cells_y, cells_z, listed, own_cell):
    starts = [jnp.zeros_like(counts[0])]
    for order in range(5):
        starts.append(starts[-1] + counts[order])
    offset = jnp.concatenate(starts[:5])
    chunk_count = (starts[5] + (ROWS - 1)) // ROWS
    frame = jnp.arange(9, dtype=jnp.int32)
    want_y = (own_cell[:, 0:1] + (frame // 3 - 1)[None] + cells_y) % cells_y
    want_z = (own_cell[:, 1:2] + (frame % 3 - 1)[None] + cells_z) % cells_z
    want = want_y + cells_y * want_z
    have = cell[0] + cells_y * cell[1]
    hit = (want[:, :, None] == have[None, None, :]) & listed[:, None, :]
    ids = jnp.arange(have.shape[0], dtype=jnp.int32)
    column = jnp.sum(jnp.where(hit, ids[None, None], 0), axis=2).astype(jnp.int32)
    return offset, chunk_count, column.reshape(-1)


def per_device(particles, counts, pairs):
    blocks = particles.shape[0]
    cross = lax.axis_size("cross")
    slab_blk = blocks * cross
    cells_z = slab_blk // GY
    local, own_cell = localize(particles, counts)
    listed = jnp.any(pairs[:, :, None] - 2 * slab_blk == jnp.arange(slab_blk, dtype=jnp.int32), axis=1)
    notes = jnp.concatenate([own_cell.T, counts[None].astype(F32), jnp.zeros((5, blocks), F32)], axis=0)
    notes = jnp.pad(notes, ((0, 0), (0, ROWS - blocks)))
    shipped = jnp.concatenate([local, notes[None]], axis=0)
    far = [passed_along(shipped, "flow", -slab) for slab in (-2, 2)]
    here, *far = lax.optimization_barrier((lax.all_gather(shipped, "cross", axis=0), *far))
    back, ahead = passed_along(here, "flow", 1), passed_along(here, "flow", -1)
    far = lax.all_gather(jnp.stack(far), "cross", axis=0)
    slabs = [far[:, 0], back, here, ahead, far[:, 1]]

    def note(value, line):
        return value[:, blocks, line, :blocks].astype(jnp.int32).reshape(slab_blk)

    slab_counts = jnp.stack([note(value, 2) for value in slabs])
    offset, chunk_count, column = tables(
        (note(here, 0), note(here, 1)), slab_counts, GY, cells_z, listed, own_cell.astype(jnp.int32)
    )
    raws = [value.reshape((-1,) + local.shape[1:]) for value in (far, back, here, ahead)]
    return pair_sums(local, raws, counts, offset, chunk_count, column)


def solution(mesh):
    placed = (P(("flow", "cross"), None, None), P(("flow", "cross")), P(("flow", "cross"), None))
    return jax.shard_map(
        per_device,
        mesh=mesh,
        in_specs=placed,
        out_specs=P(("flow", "cross"), None, None),
        check_vma=False,
    )
```

```python
import functools
import math

import jax
import jax.numpy as jnp
from jax import lax
from jax.experimental import pallas as pl
from jax.experimental.pallas import tpu as pltpu
from jax.sharding import PartitionSpec as P

GY = 8
OFFS = (-2, -1, 0, 1, 2)
kernel_coef = 5.0 * 21.0 / (16.0 * math.pi)
F32 = jnp.float32
BF16 = jnp.bfloat16
NT = (((1,), (1,)), ((), ()))
GROUP = 16
HEAD = 2
LEAD = 1
TOGETHER = 8
PIECE = 32
ROWS = 128


def passed_along(value, axis, steps):
    count = lax.axis_size(axis)
    pairs = [(source, (source + steps) % count) for source in range(count)]
    return lax.ppermute(value, axis, pairs)


def split2(value):
    high = value.astype(BF16).astype(F32)
    return high, value - high


def split3(value):
    high, rest = split2(value)
    mid, low = split2(rest)
    return high, mid, low


def three_sum(value):
    return value[0:1] + value[1:2] + value[2:3]


def rows8():
    return lax.broadcasted_iota(jnp.int32, (8, ROWS), 0)


def lane_features(field):
    row = rows8()
    high, mid = split2(field)
    velocity = pltpu.roll(field, 5, 0)
    norm = jnp.broadcast_to(three_sum(field * field), (8, ROWS))
    cross = jnp.broadcast_to(three_sum(field * velocity), (8, ROWS))
    nh, nm, nl = split3(norm)
    bh, bm, bl = split3(cross)
    xh = jnp.where(row < 3, high, pltpu.roll(high, 3, 0))
    xm = jnp.where(row < 3, mid, pltpu.roll(mid, 3, 0))
    uh = jnp.where(row < 3, pltpu.roll(high, 5, 0), 0.0)
    um = jnp.where(row < 3, pltpu.roll(mid, 5, 0), 0.0)

    def with_tail(body, six, seven):
        return jnp.where(row == 6, six, jnp.where(row == 7, seven, body))

    features = jnp.concatenate(
        [
            with_tail(xh, 1.0, 1.0),
            with_tail(xm, 1.0, nh),
            with_tail(xh, nm, nl),
            with_tail(xm, bh, bm),
            with_tail(uh, bl, 0.0),
            um,
            uh,
            jnp.zeros((8, ROWS), F32),
        ],
        axis=0,
    )
    volume = jnp.broadcast_to(field[7:8], (8, ROWS))
    density = jnp.broadcast_to(field[6:7], (8, ROWS))
    plain = jnp.where(row == 7, volume, field * volume)
    second_set = jnp.where(row < 3, plain * density, cross * volume)
    ph, pm = split2(plain)
    sh, sm = split2(second_set)
    weights = jnp.concatenate([ph, pm, sh, sm], axis=0)
    return features.astype(BF16).T, weights.astype(BF16)


def row_features(field, frame):
    row = rows8()
    step_y, step_z = 2.0 * (frame // 3 - 1), 2.0 * (frame % 3 - 1)
    field = field - jnp.where(row == 1, step_y, jnp.where(row == 2, step_z, 0.0))
    high, mid = split2(field)
    velocity = pltpu.roll(field, 5, 0)
    norm = jnp.broadcast_to((three_sum(field * field) + 0.01) * 0.25, (8, ROWS))
    cross = jnp.broadcast_to(three_sum(field * velocity), (8, ROWS))
    nh, nm, nl = split3(norm)
    ah, am, al = split3(cross)
    first = jnp.where(row < 3, -0.5, 0.0)
    second = jnp.where((row >= 3) & (row < 6), -1.0, 0.0)
    third = jnp.where(row < 3, -1.0, 0.0)
    hf, mf = high * first, mid * first
    hs, ms = high * second, mid * second
    ht, mt = high * third, mid * third
    near = jnp.concatenate(
        [
            jnp.where(row == 6, nh, jnp.where(row == 7, nm, hf)),
            jnp.where(row == 6, nl, jnp.where(row == 7, 0.25, hf)),
            jnp.where(row >= 6, 0.25, mf),
            mf,
        ],
        axis=0,
    )
    closing = jnp.concatenate(
        [
            jnp.where(row == 6, ah, jnp.where(row == 7, am, hs)),
            jnp.where(row == 6, al, hs),
            ms,
            jnp.where(row >= 6, 1.0, ms),
            jnp.where(row == 6, 1.0, ht),
            ht,
            mt,
            jnp.zeros((8, ROWS), F32),
        ],
        axis=0,
    )
    return near.astype(BF16), closing.astype(BF16)


def kernel(blocks, slab_blk, own_count, offset, chunk_count, column, own_ref, *refs):
    slab_refs, out_ref, (source, weight, near, closing), scratch = refs[:5], refs[5], refs[6:10], refs[10:]
    packs, (pre, pair_k, pair_e, pair_d, acc_k, acc_e, acc_d) = scratch[:TOGETHER], scratch[TOGETHER:]
    lane8 = lax.broadcasted_iota(jnp.int32, (8, ROWS), 1)
    row = rows8()

    def make_targets(t, carry):
        field = own_ref[t]
        for frame in range(9):
            near[t * 9 + frame], closing[t * 9 + frame] = row_features(field, frame)
        return carry

    lax.fori_loop(0, blocks, make_targets, 0)

    def make_sources(n, carry):
        firsts = [n * TOGETHER + m for m in range(TOGETHER)]
        for order, slab in enumerate(OFFS):
            for c, packed in zip(firsts, packs):
                part, place = lax.div(c, blocks), lax.rem(c, blocks)
                field = slab_refs[order][part * (blocks + 1) + place]
                field = field + jnp.where(row == 0, float(slab), 0.0)
                start = offset[order * slab_blk + c]
                inside = lax.rem(start, ROWS)
                slot = lax.div(start, ROWS)
                turned = pltpu.roll(field, inside, 1)
                here = lane8 >= inside
                packed[slot] = jnp.where(here, turned, packed[slot])
                packed[slot + 1] = jnp.where(here, 0.0, turned)

        def build(c, packed, k):
            source[c * 5 + k], weight[c * 5 + k] = lane_features(packed[k])

        for k in range(3):
            for c, packed in zip(firsts, packs):
                build(c, packed, k)

        for c, packed in zip(firsts, packs):
            @pl.when(chunk_count[c] > 3)
            def _():
                build(c, packed, 3)
                build(c, packed, 4)

        return carry

    for packed in packs:
        packed[...] = jnp.zeros_like(packed)
    lax.fori_loop(0, slab_blk // TOGETHER, make_sources, 0)

    pre[...] = jnp.ones_like(pre)
    pair_k[...] = jnp.zeros_like(pair_k)
    pair_e[...] = jnp.zeros_like(pair_e)
    pair_d[...] = jnp.zeros_like(pair_d)
    acc_k[...] = jnp.zeros_like(acc_k)
    acc_e[...] = jnp.zeros_like(acc_e)
    acc_d[...] = jnp.zeros_like(acc_d)

    frame9 = lax.broadcasted_iota(jnp.int32, (9, ROWS), 0)
    shift_y = (2 * (frame9 // 3 - 1)).astype(F32)
    shift_z = (2 * (frame9 % 3 - 1)).astype(F32)
    zero_near = jnp.zeros((32, ROWS), BF16)
    zero_weight = jnp.zeros((16, ROWS), BF16)

    def finish(t):
        half = lax.rem(t, 2)
        field = own_ref[t]

        def from_k(m):
            at = half * 288 + m
            return acc_k[pl.ds(at, 9, stride=32), :] + acc_k[pl.ds(at + 8, 9, stride=32), :]

        def from_e(m):
            at = half * 288 + m
            return acc_e[pl.ds(at, 9, stride=32), :] + acc_e[pl.ds(at + 8, 9, stride=32), :]

        def from_d(m):
            at = half * 144 + m
            return acc_d[pl.ds(at, 9, stride=16), :] + acc_d[pl.ds(at + 8, 9, stride=16), :]

        def wide(m):
            return jnp.broadcast_to(field[m:m + 1], (9, ROWS))

        place = [wide(0), wide(1) - shift_y, wide(2) - shift_z]
        speed = [wide(3), wide(4), wide(5)]
        excess = wide(6)
        s_0, s_rho, s_cross = from_k(7), from_k(6), from_k(19)
        s_x = [from_k(a) for a in range(3)]
        s_u = [from_k(3 + a) for a in range(3)]
        s_rx = [from_k(16 + a) for a in range(3)]
        e_0 = from_e(7)
        e_x = [from_e(a) for a in range(3)]
        d_0, d_rho = from_d(7), from_d(6)
        own_cross = place[0] * speed[0] + place[1] * speed[1] + place[2] * speed[2]
        close = own_cross * s_0 + s_cross
        for a in range(3):
            close = close - speed[a] * s_x[a] - place[a] * s_u[a]
        spread = (s_rho - excess * s_0) - 0.0025 * (d_rho - excess * d_0)
        results = [-(1.0 + excess) * close + 1.2 * spread]
        for a in range(3):
            pressure = excess * (place[a] * s_0 - s_x[a]) + place[a] * s_rho - s_rx[a]
            viscous = place[a] * e_0 - e_x[a]
            results.append(36.0 * pressure - 0.15 * viscous)
        live = lax.broadcasted_iota(jnp.int32, (1, ROWS), 1) < own_count[t]
        rho = 1.0 + field[6:7]
        for a in range(4):
            value = kernel_coef * jnp.sum(results[a], axis=0, keepdims=True)
            value = value if a == 0 else value / rho
            out_ref[t, a:a + 1, :] = jnp.where(live, value, 0.0)
        at = pl.multiple_of(half * 288, 32)
        acc_k[pl.ds(at, 288), :] = jnp.zeros((288, ROWS), F32)
        acc_e[pl.ds(at, 288), :] = jnp.zeros((288, ROWS), F32)
        at = pl.multiple_of(half * 144, 16)
        acc_d[pl.ds(at, 144), :] = jnp.zeros((144, ROWS), F32)

    def phase(state, side):
        t, f, k, heads, olds = state

        def advance():
            nonlocal t, f, k
            inside = jnp.minimum(t, blocks - 1)
            c = column[inside * 9 + f]
            where = c * 5 + k
            frame = inside * 9 + f
            right = jnp.concatenate(
                [jnp.concatenate([near[frame], zero_near], axis=0), closing[frame]], axis=1
            )
            both_ends = jnp.dot(source[where], right, preferred_element_type=F32)
            item = (jnp.where(t < blocks, lax.rem(t, 2) * 9 + f, 18), where, t)
            done = k + 1 >= chunk_count[c]
            k = jnp.where(done, 0, k + 1)
            f = jnp.where(done, f + 1, f)
            over = f > 8
            t = jnp.where(over, jnp.minimum(t + 1, blocks), t)
            f = jnp.where(over, 0, f)
            return both_ends, item

        news = list(heads)
        ready = [pre[side, u] for u in range(HEAD)]

        def lead():
            both_ends, item = advance()
            ready.append(both_ends)
            news.append(item)

        for u in range(LEAD):
            lead()
        for u in range(GROUP):
            both_ends = ready[u]
            if len(ready) < GROUP:
                lead()
            for low in range(0, ROWS, PIECE):
                part = slice(low, low + PIECE)
                rest = slice(ROWS + low, ROWS + low + PIECE)
                s = both_ends[part, 0:ROWS]
                e = both_ends[part, ROWS:2 * ROWS]
                inv = lax.rsqrt(s)
                w = jnp.maximum(1.0 - s * inv, 0.0)
                cube = w * w * w
                near_k = cube * (inv * inv)
                damp = near_k * e
                kh = cube.astype(BF16)
                dh = damp.astype(BF16)
                pair_k[side, u, part] = kh
                pair_k[side, u, rest] = (cube - kh.astype(F32)).astype(BF16)
                pair_e[side, u, part] = dh
                pair_e[side, u, rest] = (damp - dh.astype(F32)).astype(BF16)
                half = (u % 2) * ROWS + low
                pair_d[side, u // 2, half:half + PIECE] = near_k.astype(BF16)
            slot, where, _ = olds[u]
            w = weight[where]
            right = jnp.concatenate([pair_k[1 - side, u], pair_e[1 - side, u]], axis=1)
            total = jnp.dot(jnp.concatenate([w, w], axis=1), right, preferred_element_type=F32)
            at = pl.multiple_of(slot * 32, 32)
            acc_k[pl.ds(at, 32), :] += total[:, 0:ROWS]
            acc_e[pl.ds(at, 32), :] += total[:, ROWS:2 * ROWS]
            if u % 2:
                before = weight[olds[u - 1][1]]
                both = jnp.concatenate(
                    [
                        jnp.concatenate([before[0:16], zero_weight], axis=1),
                        jnp.concatenate([zero_weight, w[0:16]], axis=1),
                    ],
                    axis=0,
                )
                total = jnp.dot(both, pair_d[1 - side, u // 2], preferred_element_type=F32)
                at = pl.multiple_of(olds[u - 1][0] * 16, 16)
                acc_d[pl.ds(at, 16), :] += total[0:16]
                at = pl.multiple_of(slot * 16, 16)
                acc_d[pl.ds(at, 16), :] += total[16:32]
        heads = []
        for u in range(HEAD):
            both_ends, item = advance()
            pre[1 - side, u] = both_ends
            heads.append(item)
        return t, f, k, tuple(heads), tuple(news)

    def step(state):
        for side in range(2):
            olds = state[4]
            state = phase(state, side)

            @pl.when(state[4][0][2] > olds[0][2])
            def _():
                finish(olds[0][2])

        return state

    zero = jnp.int32(0)
    idle = tuple((jnp.int32(18), zero, zero) for _ in range(GROUP))
    lax.while_loop(lambda state: state[4][0][2] < blocks, step, (zero, zero, zero, idle[:HEAD], idle))


def pair_sums(own, raws, own_count, offset, chunk_count, column):
    blocks = own.shape[0]
    slab_blk = chunk_count.shape[0]
    chunks = slab_blk * 5
    smem = pl.BlockSpec(memory_space=pltpu.SMEM)
    vmem = pl.BlockSpec(memory_space=pltpu.VMEM)
    return pl.pallas_call(
        functools.partial(kernel, blocks, slab_blk),
        out_shape=jax.ShapeDtypeStruct((blocks, 4, ROWS), F32),
        in_specs=[smem] * 4 + [vmem] * 6,
        out_specs=vmem,
        scratch_shapes=[
            pltpu.VMEM((chunks, ROWS, 64), BF16),
            pltpu.VMEM((chunks, 32, ROWS), BF16),
            pltpu.VMEM((blocks * 9, 32, ROWS), BF16),
            pltpu.VMEM((blocks * 9, 64, ROWS), BF16),
            *[pltpu.VMEM((7, 8, ROWS), F32) for _ in range(TOGETHER)],
            pltpu.VMEM((2, HEAD, ROWS, 2 * ROWS), F32),
            pltpu.VMEM((2, GROUP, 2 * ROWS, ROWS), BF16),
            pltpu.VMEM((2, GROUP, 2 * ROWS, ROWS), BF16),
            pltpu.VMEM((2, GROUP // 2, 2 * ROWS, ROWS), BF16),
            pltpu.VMEM((19 * 32, ROWS), F32),
            pltpu.VMEM((19 * 32, ROWS), F32),
            pltpu.VMEM((19 * 16, ROWS), F32),
        ],
        name="pair_sums",
    )(own_count, offset, chunk_count, column, own, *raws)


def localize(particles, counts):
    slots = particles.shape[2]
    live = lax.broadcasted_iota(jnp.int32, (1, slots), 1) < counts[:, None]
    lowest = jnp.min(jnp.where(live[:, None], particles[:, 1:3], 1e9), axis=2)
    cell = jnp.floor(lowest * 0.5)
    centre = 2.0 * cell + 1.0
    fields = jnp.stack(
        [
            particles[:, 0] - 0.5,
            particles[:, 1] - centre[:, 0:1],
            particles[:, 2] - centre[:, 1:2],
            particles[:, 3],
            particles[:, 4],
            particles[:, 5],
            particles[:, 6] - 1.0,
            particles[:, 7] / particles[:, 6],
        ],
        axis=1,
    )
    return jnp.where(live[:, None], fields, 0.0), cell


def tables(cell, counts, cells_y, cells_z, listed, own_cell):
    starts = [jnp.zeros_like(counts[0])]
    for order in range(5):
        starts.append(starts[-1] + counts[order])
    offset = jnp.concatenate(starts[:5])
    chunk_count = (starts[5] + (ROWS - 1)) // ROWS
    frame = jnp.arange(9, dtype=jnp.int32)
    want_y = (own_cell[:, 0:1] + (frame // 3 - 1)[None] + cells_y) % cells_y
    want_z = (own_cell[:, 1:2] + (frame % 3 - 1)[None] + cells_z) % cells_z
    want = want_y + cells_y * want_z
    have = cell[0] + cells_y * cell[1]
    hit = (want[:, :, None] == have[None, None, :]) & listed[:, None, :]
    ids = jnp.arange(have.shape[0], dtype=jnp.int32)
    column = jnp.sum(jnp.where(hit, ids[None, None], 0), axis=2).astype(jnp.int32)
    return offset, chunk_count, column.reshape(-1)


def per_device(particles, counts, pairs):
    blocks = particles.shape[0]
    cross = lax.axis_size("cross")
    slab_blk = blocks * cross
    cells_z = slab_blk // GY
    local, own_cell = localize(particles, counts)
    listed = jnp.any(pairs[:, :, None] - 2 * slab_blk == jnp.arange(slab_blk, dtype=jnp.int32), axis=1)
    notes = jnp.concatenate([own_cell.T, counts[None].astype(F32), jnp.zeros((5, blocks), F32)], axis=0)
    notes = jnp.pad(notes, ((0, 0), (0, ROWS - blocks)))
    shipped = jnp.concatenate([local, notes[None]], axis=0)
    far = [passed_along(shipped, "flow", -slab) for slab in (-2, 2)]
    here, *far = lax.optimization_barrier((lax.all_gather(shipped, "cross", axis=0), *far))
    back, ahead = passed_along(here, "flow", 1), passed_along(here, "flow", -1)
    behind, after = lax.optimization_barrier((lax.all_gather(far[0], "cross", axis=0), far[1]))
    slabs = [behind, back, here, ahead, lax.all_gather(after, "cross", axis=0)]

    def note(value, line):
        return value[:, blocks, line, :blocks].astype(jnp.int32).reshape(slab_blk)

    slab_counts = jnp.stack([note(value, 2) for value in slabs])
    offset, chunk_count, column = tables(
        (note(here, 0), note(here, 1)), slab_counts, GY, cells_z, listed, own_cell.astype(jnp.int32)
    )
    raws = [value.reshape((-1,) + local.shape[1:]) for value in slabs]
    return pair_sums(local, raws, counts, offset, chunk_count, column)


def solution(mesh):
    placed = (P(("flow", "cross"), None, None), P(("flow", "cross")), P(("flow", "cross"), None))
    return jax.shard_map(
        per_device,
        mesh=mesh,
        in_specs=placed,
        out_specs=P(("flow", "cross"), None, None),
        check_vma=False,
    )
```
